32 devices in a mesh: slab: 2 (over y), col: 4 (over z), row: 2 (over x), ch: 2 (over core).
Axes of the slice: x: 2, y: 2, z: 4, core: 2. Of those that a mesh axis runs over, the one named last changes fastest.
Arguments:
- left_feat: bfloat16 [128, 128, 1024], P(('slab', 'row'), 'ch', 'col'), parts along dimension 0, may hold values from -512 to 512
- right_feat: bfloat16 [128, 128, 1024], P(('slab', 'row'), 'ch', 'col'), parts along dimension 0, may hold values from -12 to 12
- offsets: int32 [8], P(('slab', 'col')), parts along dimension 0, may hold values from 0 to 256, as said below
- valid: int32 [128, 1024], P(('slab', 'row'), ('col', 'ch')), parts along dimension 0, may hold values 0 or 1
- w_first: float32 [3, 3, 32, 2], replicated, may hold values from -1.5 to 1.5
- w_middle: float32 [3, 3, 32, 32], replicated, may hold values from -0.375 to 0.375
- w_last: float32 [3, 3, 1, 32], replicated, may hold values from -0.375 to 0.375
- grad_out: float32 [128, 1024], P(('slab', 'row'), ('col', 'ch')), parts along dimension 0, may hold values from -6 to 6
Outputs:
- refined: float32 [128, 1024], P(('slab', 'row'), ('col', 'ch')), parts along dimension 0
- grad_left: bfloat16 [128, 128, 1024], P(('slab', 'row'), 'ch', 'col'), parts along dimension 0
- grad_right: bfloat16 [128, 128, 1024], P(('slab', 'row'), 'ch', 'col'), parts along dimension 0
The draws below stay inside these ranges and needn't reach their ends.
There are 2 independent parts, one for each index of `slab`. The reference program is written for one: setup_inputs(seed, part) draws one part's arguments, and reference() takes and returns one part's arrays. A program takes and returns all parts, laid end to end along the dimension named above; an argument that names none is the same for every part. Nothing has to cross between parts.
Inputs may be any that keep to these rules, and one draw needn't show every extreme that they name: `offsets`: the largest tile offset is exactly 256 in every draw.
All inputs are finite; a program needn't handle non-finite values. No bound on the sum of `valid` on one device may be relied on, other than what follows from the above.
Results may differ from the reference program's by a relative error of at most 0.005.
Values may be sent and summed in bfloat16 or wider, within the bound.
No kernel may reach another device: no remote copies, remote signals or barrier semaphores. Data moves between devices by JAX's collectives and lax.ppermute only.
A program may use at most 128 MiB of HBM per device.

```python
import math
import jax
import jax.numpy as jnp
from jax import lax

FEAT = 128
DISP = 256
REFINE = 32
W_DEV = 256
H = 64
COL_TILES = 4
W = 1024
OFFMAX = 256


def band_offsets(key):
    base_key = jax.random.fold_in(key, 11)
    values = jax.random.randint(base_key, (COL_TILES,), 0, OFFMAX + 1, dtype=jnp.int32)
    chosen = jax.random.randint(jax.random.fold_in(base_key, 1), (), 0, COL_TILES, dtype=jnp.int32)
    return jnp.where(jnp.arange(COL_TILES, dtype=jnp.int32) == chosen, OFFMAX, values).astype(jnp.int32)


def feature_pair(key):
    right_vals = jax.random.normal(jax.random.fold_in(key, 21), (H, W, FEAT), jnp.float32)
    left_vals = jax.random.normal(jax.random.fold_in(key, 22), (H, W, FEAT), jnp.float32)
    left_out = jnp.transpose(jnp.clip(left_vals, -512.0, 512.0), (0, 2, 1))
    right_out = jnp.transpose(jnp.clip(right_vals, -12.0, 12.0), (0, 2, 1))
    return (left_out, right_out)


def draw_left_feat(key, part):
    return feature_pair(key)[0].astype(jnp.bfloat16)


def draw_right_feat(key, part):
    return feature_pair(key)[1].astype(jnp.bfloat16)


def draw_offsets(key, part):
    return band_offsets(key)


def with_ends(entries, rng, low, top_value):
    index_at = [jax.random.randint(jax.random.fold_in(rng, axis), (), 0, length) for axis, length in enumerate(entries.shape)]
    main_axis = entries.shape.index(max(entries.shape))
    beside = index_at[:main_axis] + [(index_at[main_axis] + 1) % entries.shape[main_axis]] + index_at[main_axis + 1:]
    return entries.at[tuple(index_at)].set(low).at[tuple(beside)].set(top_value)


def block_levels(key, dims, split, low, top_value):
    loudness = 1.0
    for dim, shards_of in split:
        draws = jax.random.uniform(jax.random.fold_in(jax.random.fold_in(key, 6), dim), (shards_of,), jnp.float32, low / len(split), top_value / len(split))
        loudness = loudness * jnp.repeat(jnp.exp(draws), dims[dim] // shards_of).reshape((-1,) + (1,) * (len(dims) - 1 - dim))
    return loudness


def scatter_about(stream_key, shape, deviation, most, cuts=(), kind=jnp.bfloat16):
    loudness = block_levels(stream_key, shape, cuts, -0.22, 0.18) if cuts else 1.0
    array = jax.random.normal(stream_key, shape, jnp.float32) * deviation * loudness
    return jnp.minimum(jnp.maximum(array, -most), most).astype(kind)


def setup_inputs(seed: int = 0, part: int = 0) -> dict:
    streams_of = jax.random.split(jax.random.key(seed), 9)
    part_keys = jax.random.split(jax.random.fold_in(streams_of[8], part), 9)
    return {
        "left_feat": draw_left_feat(jax.random.fold_in(jax.random.fold_in(streams_of[8], part), 71), part),
        "right_feat": draw_right_feat(jax.random.fold_in(jax.random.fold_in(streams_of[8], part), 71), part),
        "offsets": draw_offsets(jax.random.fold_in(jax.random.fold_in(streams_of[8], part), 71), part),
        "valid": with_ends((jax.random.randint(part_keys[3], (H, W), 0, 8) < 7).astype(jnp.int32), jax.random.fold_in(part_keys[3], 1), 0, 1),
        "w_first": scatter_about(streams_of[4], (3, 3, REFINE, 2), 18 ** -0.5, 1.5, (), jnp.float32),
        "w_middle": scatter_about(streams_of[5], (3, 3, REFINE, REFINE), (9 * REFINE) ** -0.5, 0.375, (), jnp.float32),
        "w_last": scatter_about(streams_of[6], (3, 3, 1, REFINE), (9 * REFINE) ** -0.5, 0.375, (), jnp.float32),
        "grad_out": scatter_about(part_keys[7], (H, W), 1.0, 6.0, ((0, 2), (1, 8)), jnp.float32),
    }


def skew_out(products):
    tile_rows, band_span = products.shape
    flat_rows = jnp.concatenate([products.reshape(-1), jnp.zeros((tile_rows,), products.dtype)])
    return flat_rows.reshape(tile_rows, band_span + 1)[:, 1:DISP + 1]

def skew_in(band_vals, band_span):
    tile_rows = band_vals.shape[0]
    padded = jnp.pad(band_vals, ((0, 0), (1, band_span - DISP)))
    return padded.reshape(-1)[:tile_rows * band_span].reshape(tile_rows, band_span)

def band_stats(scores, offset_term):
    probs = jax.nn.softmax(scores, axis=-1)
    levels = (DISP - 1 - jnp.arange(DISP).astype(jnp.float32)) / DISP
    mean_level = lax.optimization_barrier(jnp.sum(probs * levels, axis=-1))
    coarse = offset_term / DISP + mean_level
    spread = lax.optimization_barrier(jnp.sum(probs * (levels - mean_level[..., None]) ** 2, axis=-1))
    return (coarse, spread)

def conv_taps(padded, weights, rows_out, cols_out):
    result = jnp.zeros((weights.shape[2], rows_out, cols_out), jnp.float32)
    for tap_row in range(3):
        for tap_col in range(3):
            result = result + jnp.einsum('oi,ihw->ohw', weights[tap_row, tap_col], padded[:, tap_row:tap_row + rows_out, tap_col:tap_col + cols_out], precision=lax.Precision.HIGHEST)
    return result

def conv_same(field, weights):
    padded = jnp.pad(field, ((0, 0), (1, 1), (1, 1)))
    return conv_taps(padded, weights, field.shape[1], field.shape[2])

def refine(coarse, spread, valid_f, w_first, w_middle, w_last):
    inputs = jnp.stack([coarse * valid_f, spread * valid_f])
    hidden_one = jax.nn.silu(conv_same(inputs, w_first))
    hidden_two = jax.nn.silu(conv_same(hidden_one, w_middle))
    return valid_f * (coarse + conv_same(hidden_two, w_last)[0])

def reference(left_feat, right_feat, offsets, valid, w_first, w_middle, w_last, grad_out):
    left_feat = jnp.transpose(left_feat, (0, 2, 1))
    right_feat = jnp.transpose(right_feat, (0, 2, 1))
    pad_left = OFFMAX + DISP
    band_span = W_DEV + DISP
    right_pad = jnp.pad(right_feat, ((0, 0), (pad_left, 0), (0, 0)))
    tile_ids = jnp.arange(COL_TILES).astype(jnp.int32)
    row_ids = jnp.arange(H).astype(jnp.int32)

    def tile_inputs(row_index, tile_index):
        left_row = lax.dynamic_index_in_dim(left_feat, row_index, 0, keepdims=False)
        right_row = lax.dynamic_index_in_dim(right_pad, row_index, 0, keepdims=False)
        left_tile = lax.dynamic_slice_in_dim(left_row, (tile_index * W_DEV).astype(jnp.int32), W_DEV, 0)
        start_col = (tile_index * W_DEV - offsets[tile_index] - DISP + pad_left).astype(jnp.int32)
        right_band = lax.dynamic_slice_in_dim(right_row, start_col, band_span, 0)
        return (left_tile, right_band, start_col)

    def cost_row(row_index):

        def cost_tile(tile_index):
            left_tile, right_band, start_col = tile_inputs(row_index, tile_index)
            products = jnp.dot(left_tile, right_band.T, preferred_element_type=jnp.float32)
            return skew_out(products)
        return lax.map(cost_tile, tile_ids).reshape(W, DISP)
    cost = lax.map(cost_row, row_ids)
    offset_cols = jnp.repeat(offsets, W_DEV).astype(jnp.float32)
    valid_f = valid.astype(jnp.float32)
    (coarse, spread), stats_back = jax.vjp(lambda scores: band_stats(scores, offset_cols), cost / math.sqrt(FEAT))
    refined, refine_back = jax.vjp(lambda first_in, second_in: refine(first_in, second_in, valid_f, w_first, w_middle, w_last), coarse, spread)
    grad_coarse, grad_spread = refine_back(grad_out)
    grad_scores = stats_back((grad_coarse, grad_spread))[0]
    grad_cost = (grad_scores / math.sqrt(FEAT)).astype(jnp.bfloat16)

    def grad_row(row_index):
        grad_cost_row = lax.dynamic_index_in_dim(grad_cost, row_index, 0, keepdims=False)

        def tile_step(carry, tile_index):
            left_tile, right_band, start_col = tile_inputs(row_index, tile_index)
            band_vals = lax.dynamic_slice_in_dim(grad_cost_row, (tile_index * W_DEV).astype(jnp.int32), W_DEV, 0)
            band_grad = skew_in(band_vals, band_span)
            left_grad = jnp.dot(band_grad, right_band, preferred_element_type=jnp.float32)
            right_grad = jnp.dot(band_grad.T, left_tile, preferred_element_type=jnp.float32)
            updated = lax.dynamic_slice_in_dim(carry, start_col, band_span, 0) + right_grad
            carry = lax.dynamic_update_slice_in_dim(carry, updated, start_col, 0)
            return (carry, left_grad)
        carry_init = jnp.zeros((pad_left + W, FEAT), jnp.float32)
        final_carry, left_tiles = lax.scan(tile_step, carry_init, tile_ids)
        return (left_tiles.reshape(W, FEAT), final_carry[pad_left:])
    grad_left_all, grad_right_all = lax.map(grad_row, row_ids)
    grad_left_out = jnp.transpose(grad_left_all.astype(jnp.bfloat16), (0, 2, 1))
    grad_right_out = jnp.transpose(grad_right_all.astype(jnp.bfloat16), (0, 2, 1))
    return (refined, grad_left_out, grad_right_out)
```

```python
import functools
import math

import jax
import jax.numpy as jnp
import numpy as np
from jax import lax
from jax.experimental import pallas as pl
from jax.experimental.pallas import tpu as pltpu
from jax.sharding import PartitionSpec as P

DISP = 256
HALO = 4
LANES = 128
SIDE = 128
ALIGN = 16
NEG = -1e30
BAND = 400
GROUP = 4
F32 = jnp.float32
BF16 = jnp.bfloat16


def dot(a, b, dims=((1,), (0,))):
    return lax.dot_general(a, b, (dims, ((), ())), preferred_element_type=F32)


def band_tables(off):
    rem = (DISP + 1 - off) % ALIGN
    across = lax.broadcasted_iota(jnp.int32, (BAND, LANES), 1)
    down = lax.broadcasted_iota(jnp.int32, (BAND, LANES), 0)
    delta = across - down + (DISP - 1) + rem
    inside = (delta >= 0) & (delta < DISP)
    return delta.astype(F32) / DISP, jnp.where(inside, 0.0, NEG).astype(F32)


def band_start(off, block):
    rem = (DISP + 1 - off) % ALIGN
    return pl.multiple_of(LANES * block + DISP + 1 - off - rem, ALIGN)


def stats_body(chans, off_ref, lk, lo, r0k, r0o, r1k, r1o, r2k, r2o, grad_ref, keep_ref,
               field, top, bottom, stats, cost, level, mask, lines):
    step = pl.program_id(0)
    rate = math.log2(math.e) / math.sqrt(chans)
    off = off_ref[0]
    width = lk.shape[2]

    @pl.when(step == 0)
    def _():
        lev, msk = band_tables(off)
        level[...] = lev
        mask[...] = msk
        cost[3 * width:, :] = jnp.zeros((cost.shape[0] - 3 * width, width), F32)

    @pl.loop(0, GROUP)
    def _(row):
        left = jnp.concatenate([lk[row], lo[row]], axis=0)
        for slot, (own, other) in enumerate(((r2k, r2o), (r1k, r1o), (r0k, r0o))):
            right = jnp.concatenate([own[row], other[row]], axis=0)
            cost[slot * width:(slot + 1) * width, :] = dot(right, left, ((0,), (0,)))
        line = step * GROUP + row
        for block in range(width // LANES):
            cols = slice(block * LANES, (block + 1) * LANES)
            scores = cost[pl.ds(band_start(off, block), BAND), cols] + mask[...]
            top_score = jnp.max(scores, axis=0, keepdims=True)
            weight = jnp.exp2((scores - top_score) * rate)
            lev = level[...]
            total = jnp.sum(weight, axis=0, keepdims=True)
            mean = jnp.sum(weight * lev, axis=0, keepdims=True) / total
            apart = lev - mean
            spread = jnp.sum(weight * apart * apart, axis=0, keepdims=True) / total
            for at, value in enumerate((spread, top_score, mean, 1.0 / total)):
                lines[line, at:at + 1, cols] = value

    rows = field.shape[1]

    @pl.when(step == pl.num_programs(0) - 1)
    def _():
        for line in range(rows):
            for at in range(4):
                stats[at + 1, line:line + 1, :] = lines[line, at:at + 1, :]
        keep = keep_ref[...]
        coarse = stats[3] + off.astype(F32) / DISP
        stats[0] = coarse
        field[0] = coarse * keep
        field[1] = stats[1] * keep
        field[2] = grad_ref[...] * keep
        top[...] = field[:, :HALO, :]
        bottom[...] = field[:, rows - HALO:, :]


def group_spec(array):
    return pl.BlockSpec((GROUP,) + array.shape[1:], lambda i: (i, 0, 0))


def full_spec(shape):
    return pl.BlockSpec(shape, lambda i: (0,) * len(shape))


SMEM = pl.BlockSpec(memory_space=pltpu.SMEM)


def cost_of(flops, moved):
    return pl.CostEstimate(flops=flops, bytes_accessed=moved, transcendentals=0)


def band_stats(off, left, rights, grad_out, keep):
    rows, half, width = left[0].shape
    chans = 2 * half
    feats = list(left) + [part for pair in rights for part in pair]
    small = (rows, width)
    outs = ((3,) + small, (3, HALO, width), (3, HALO, width), (5,) + small)
    return pl.pallas_call(
        functools.partial(stats_body, chans),
        name="band_stats",
        grid=(rows // GROUP,),
        in_specs=[SMEM] + [group_spec(a) for a in feats] + [full_spec(small)] * 2,
        out_specs=[full_spec(s) for s in outs],
        out_shape=[jax.ShapeDtypeStruct(s, F32) for s in outs],
        scratch_shapes=[
            pltpu.VMEM((3 * width + ALIGN, width), F32),
            pltpu.VMEM((BAND, LANES), F32),
            pltpu.VMEM((BAND, LANES), F32),
            pltpu.VMEM((rows, 8, width), F32),
        ],
        cost_estimate=cost_of(2 * rows * 3 * width * width * chans, rows * 4 * width * chans * 2),
    )(off, *feats, grad_out, keep)


def left_body(chans, off_ref, lk, lo, r0k, r0o, r1k, r1o, r2k, r2o, coef, out_own, out_other,
              cost, slopes, level, mask):
    step = pl.program_id(0)
    rate = math.log2(math.e) / math.sqrt(chans)
    off = off_ref[0]
    width = lk.shape[2]

    @pl.when(step == 0)
    def _():
        lev, msk = band_tables(off)
        level[...] = lev
        mask[...] = msk
        cost[3 * width:, :] = jnp.zeros((cost.shape[0] - 3 * width, width), F32)
        slopes[...] = jnp.zeros(slopes.shape, BF16)

    @pl.loop(0, GROUP)
    def _(row):
        left = jnp.concatenate([lk[row], lo[row]], axis=0)
        rights = [jnp.concatenate([own[row], other[row]], axis=0)
                  for own, other in ((r2k, r2o), (r1k, r1o), (r0k, r0o))]
        for slot, right in enumerate(rights):
            cost[slot * width:(slot + 1) * width, :] = dot(right, left, ((0,), (0,)))
        at = step * GROUP + row
        for block in range(width // LANES):
            cols = slice(block * LANES, (block + 1) * LANES)
            where = pl.ds(band_start(off, block), BAND)
            top_score, mean, one, two, three = (coef[at, f:f + 1, cols] for f in range(5))
            weight = jnp.exp2((cost[where, cols] + mask[...] - top_score) * rate)
            apart = level[...] - mean
            slopes[where, cols] = (weight * (apart * (one + two * apart) - three)).astype(BF16)
        total = sum(dot(right, slopes[slot * width:(slot + 1) * width, :])
                    for slot, right in enumerate(rights))
        out_own[row] = total[:chans // 2].astype(BF16)
        out_other[row] = total[chans // 2:].astype(BF16)


def left_grads(off, left, rights, coef):
    rows, half, width = left[0].shape
    chans = 2 * half
    feats = list(left) + [part for pair in rights for part in pair]
    return pl.pallas_call(
        functools.partial(left_body, chans),
        name="left_grads",
        grid=(rows // GROUP,),
        in_specs=[SMEM] + [group_spec(a) for a in feats] + [full_spec(coef.shape)],
        out_specs=[group_spec(left[0])] * 2,
        out_shape=[jax.ShapeDtypeStruct(left[0].shape, BF16)] * 2,
        scratch_shapes=[
            pltpu.VMEM((3 * width + ALIGN, width), F32),
            pltpu.VMEM((3 * width + ALIGN, width), BF16),
            pltpu.VMEM((BAND, LANES), F32),
            pltpu.VMEM((BAND, LANES), F32),
        ],
        cost_estimate=cost_of(4 * rows * 3 * width * width * chans, rows * 5 * width * chans * 2),
    )(off, *feats, coef)


def right_body(chans, offs_ref, rk, ro, l0k, l0o, l1, l2, coef0, coef1, coef2,
               out_own, out_other, cost, slopes, mask):
    step = pl.program_id(0)
    rate = math.log2(math.e) / math.sqrt(chans)
    width = rk.shape[2]
    parts = width // LANES
    across = lax.broadcasted_iota(jnp.int32, (LANES, LANES), 1)
    down = lax.broadcasted_iota(jnp.int32, (LANES, LANES), 0)
    blocks = [(tile, col, row) for tile in range(3) for col in range(parts) for row in range(parts)]

    def base_of(tile, col, row):
        return tile * width + (col - row) * LANES - offs_ref[tile]

    def spot(tile, col, row):
        return (slice(row * LANES, (row + 1) * LANES),
                slice(tile * width + col * LANES, tile * width + (col + 1) * LANES))

    @pl.when(step == 0)
    def _():
        slopes[...] = jnp.zeros(slopes.shape, BF16)
        for tile, col, row in blocks:
            delta = across - down + base_of(tile, col, row)
            inside = (delta >= 0) & (delta < DISP)
            mask[spot(tile, col, row)] = jnp.where(inside, 0.0, NEG).astype(F32)

    @pl.loop(0, GROUP)
    def _(line):
        right = jnp.concatenate([rk[line], ro[line]], axis=0)
        lefts = [jnp.concatenate([l0k[line], l0o[line]], axis=0), l1[line], l2[line]]
        for tile, left in enumerate(lefts):
            cost[:, tile * width:(tile + 1) * width] = dot(right, left, ((0,), (0,)))
        at = step * GROUP + line
        table = (across - down).astype(F32) / DISP
        for tile, col, row in blocks:
            base = base_of(tile, col, row)

            @pl.when((base + LANES > 0) & (base - LANES < DISP))
            def _(tile=tile, col=col, row=row, base=base):
                here = spot(tile, col, row)
                cols = slice(col * LANES, (col + 1) * LANES)
                coef = (coef0, coef1, coef2)[tile]
                top_score, mean, one, two, three = (coef[at, f:f + 1, cols] for f in range(5))
                weight = jnp.exp2((cost[here] + mask[here] - top_score) * rate)
                apart = (table + base.astype(F32) / DISP) - mean
                slopes[here] = (weight * (apart * (one + two * apart) - three)).astype(BF16)

        total = sum(dot(left, slopes[:, tile * width:(tile + 1) * width], ((1,), (1,)))
                    for tile, left in enumerate(lefts))
        out_own[line] = total[:chans // 2].astype(BF16)
        out_other[line] = total[chans // 2:].astype(BF16)


def right_grads(offs, right, left, left_one, left_two, coefs):
    rows, half, width = right[0].shape
    chans = 2 * half
    feats = list(right) + list(left) + [left_one, left_two]
    return pl.pallas_call(
        functools.partial(right_body, chans),
        name="right_grads",
        grid=(rows // GROUP,),
        in_specs=[SMEM] + [group_spec(a) for a in feats] + [full_spec(a.shape) for a in coefs],
        out_specs=[group_spec(right[0])] * 2,
        out_shape=[jax.ShapeDtypeStruct(right[0].shape, BF16)] * 2,
        scratch_shapes=[
            pltpu.VMEM((width, 3 * width), F32),
            pltpu.VMEM((width, 3 * width), BF16),
            pltpu.VMEM((width, 3 * width), F32),
        ],
        cost_estimate=cost_of(4 * rows * 3 * width * width * chans, rows * 5 * width * chans * 2),
    )(offs, *feats, *coefs)


def split_halves(values):
    high = values.astype(BF16)
    return high, (values - high.astype(F32)).astype(BF16)


def fine_dot(weights, high, low):
    w_high, w_low = weights
    return dot(w_high, high) + dot(w_high, low) + dot(w_low, high)


def tap_rows(values):
    last = values.shape[1] - 1
    return jnp.concatenate([pltpu.roll(values, 1, 1), values, pltpu.roll(values, last, 1)], axis=0)


def merge_taps(stacked):
    count, lanes = stacked.shape[0] // 3, stacked.shape[1]
    return (pltpu.roll(stacked[:count], 1, 1) + stacked[count:2 * count]
            + pltpu.roll(stacked[2 * count:], lanes - 1, 1))


def refine_body(chans, hid, flags, field, above, below, side, stats, keep_ref,
                w_one, w_two, w_three, w_three_back, w_two_back, w_one_back,
                refined, coef, wide, one_high, one_low, slope_one,
                two_high, two_low, slope_two, g_two_high, g_two_low, g_one_high, g_one_low):
    rows, width = field.shape[1:]
    ext = rows + 2 * HALO
    lanes = width + SIDE
    for f in range(3):
        base = f * ext
        wide[base:base + HALO, :width] = above[f]
        wide[base + HALO:base + HALO + rows, :width] = field[f]
        wide[base + HALO + rows:base + ext, :width] = below[f]
        wide[base:base + ext, width:] = side[f]

    def present(first, count):
        line = first + lax.broadcasted_iota(jnp.int32, (count * hid, lanes), 0) // hid
        lane = lax.broadcasted_iota(jnp.int32, (count * hid, lanes), 1)
        low = HALO * flags[0]
        high = ext - HALO * flags[1]
        start = lanes - (SIDE // 2) * (1 - flags[2])
        end = width + (SIDE // 2) * (1 - flags[3])
        return (line >= low) & (line < high) & ((lane < end) | (lane >= start))

    def gate(values):
        return 1.0 / (1.0 + jnp.exp(-values))

    def activate(values, first, count, high_ref, low_ref, slope_ref, at):
        sig = gate(values)
        ok = present(first, count)
        hidden = jnp.where(ok, values * sig, 0.0)
        slope_ref[at] = jnp.where(ok, sig * (1.0 + values * (1.0 - sig)), 0.0)
        high_ref[at], low_ref[at] = split_halves(hidden)

    piece = 6
    taps = split_halves(tap_rows(wide[:2 * ext, :]))
    for part in range(ext // piece):
        at = slice(part * piece * hid, (part + 1) * piece * hid)
        values = fine_dot(split_halves(w_one[at, :]), *taps)
        activate(values, part * piece, piece, one_high, one_low, slope_one, at)

    count = ext - 4
    wt = split_halves(w_two[...])
    piece = w_two.shape[0] // (3 * hid)
    for part in range(count // piece):
        source = slice((part * piece + 1) * hid, (part * piece + 1) * hid + w_two.shape[1])
        values = merge_taps(fine_dot(wt, one_high[source], one_low[source]))
        at = slice(part * piece * hid, (part + 1) * piece * hid)
        activate(values, part * piece + 2, piece, two_high, two_low, slope_two, at)

    inner = slice(hid, (count - 1) * hid)
    out = merge_taps(fine_dot(split_halves(w_three[...]), two_high[inner], two_low[inner]))
    keep = keep_ref[...]
    refined[...] = keep * (stats[0] + out[:, :width])

    taps = split_halves(tap_rows(wide[2 * ext:, :]))
    for part in range(count // piece):
        at = slice(part * piece * hid, (part + 1) * piece * hid)
        grads = fine_dot(split_halves(w_three_back[at, :]), *taps) * slope_two[at]
        g_two_high[at], g_two_low[at] = split_halves(grads)

    wt = split_halves(w_two_back[...])
    piece = w_two_back.shape[0] // (3 * hid)
    for part in range((count - 2) // piece):
        source = slice(part * piece * hid, part * piece * hid + w_two_back.shape[1])
        at = slice(part * piece * hid, (part + 1) * piece * hid)
        over = slice((part * piece + 3) * hid, (part * piece + 3 + piece) * hid)
        grads = merge_taps(fine_dot(wt, g_two_high[source], g_two_low[source])) * slope_one[over]
        g_one_high[at], g_one_low[at] = split_halves(grads)

    back = merge_taps(fine_dot(split_halves(w_one_back[...]), g_one_high[...], g_one_low[...]))
    for_coarse = field[2] + back[:rows, :width] * keep
    for_spread = back[rows:, :width] * keep
    scale = stats[4] / math.sqrt(chans)
    planes = (stats[2], stats[3], for_coarse * scale, for_spread * scale,
              for_spread * stats[1] * scale, jnp.full((rows, width), flags[4], jnp.int32).astype(F32))
    coef[...] = jnp.zeros(coef.shape, F32)
    for at, plane in enumerate(planes):
        for line in range(rows):
            coef[line, at:at + 1, :] = plane[line:line + 1, :]


def near(out_rows, in_rows, shift):
    gap = np.arange(in_rows)[None, :] - np.arange(out_rows)[:, None] + shift
    return [(gap == tap).astype(np.float32) for tap in range(3)]


def expand(weights, out_rows, in_rows, shift, order):
    table = near(out_rows, in_rows, shift)
    full = sum(jnp.asarray(table[tap])[None, :, None, :, None] * weights[tap][:, None, :, None, :]
               for tap in range(3))
    return jnp.transpose(full, order)


def refine_weights(w_first, w_middle, w_last, rows):
    ext = rows + 2 * HALO
    hid, ins = w_first.shape[2:]

    def turned(w):
        return jnp.transpose(w[::-1, ::-1], (0, 1, 3, 2))

    one = expand(w_first, ext, ext, 1, (1, 2, 0, 4, 3)).reshape(ext * hid, 3 * ins * ext)
    two = expand(w_middle, 5, 7, 0, (0, 1, 2, 3, 4)).reshape(3 * 5 * hid, 7 * hid)
    three = expand(w_last, rows, rows + 2, 0, (0, 1, 2, 3, 4)).reshape(3 * rows, (rows + 2) * hid)
    three_back = expand(turned(w_last), ext - 4, ext, -1, (1, 2, 0, 4, 3)).reshape(
        (ext - 4) * hid, 3 * ext)
    two_back = expand(turned(w_middle), 6, 8, 0, (0, 1, 2, 3, 4)).reshape(3 * 6 * hid, 8 * hid)
    one_back = expand(turned(w_first), rows, rows + 2, 0, (0, 2, 1, 3, 4)).reshape(
        3 * ins * rows, (rows + 2) * hid)
    return one, two, three, three_back, two_back, one_back


def refine(flags, field, above, below, side, stats, keep, weights, chans, hid):
    rows, width = field.shape[1:]
    ext, lanes = rows + 2 * HALO, width + SIDE
    small = (rows, width)
    vmem = pl.BlockSpec(memory_space=pltpu.VMEM)
    outs = (small, (rows, 8, width))

    def both(count):
        return [pltpu.VMEM((count * hid, lanes), BF16)] * 2

    def single(count):
        return [pltpu.VMEM((count * hid, lanes), F32)]

    return pl.pallas_call(
        functools.partial(refine_body, chans, hid),
        name="refine",
        in_specs=[SMEM] + [vmem] * 12,
        out_specs=[vmem] * 2,
        out_shape=[jax.ShapeDtypeStruct(s, F32) for s in outs],
        scratch_shapes=[pltpu.VMEM((3 * ext, lanes), F32)] + both(ext) + single(ext)
        + both(ext - 4) + single(ext - 4) + both(ext - 4) + both(ext - 6),
        cost_estimate=cost_of(4 * 10 ** 9, 8 * 10 ** 6),
    )(flags, field, above, below, side, stats, keep, *weights)


def shards(left_feat, right_feat, offsets, valid, w_first, w_middle, w_last, grad_out):
    cols, rows2 = lax.axis_size("col"), lax.axis_size("row") * lax.axis_size("ch")
    col, core = lax.axis_index("col"), lax.axis_index("ch")
    band = lax.axis_index("row") * lax.axis_size("ch") + core
    chans = left_feat.shape[1] * lax.axis_size("ch")
    hid = w_first.shape[2]
    rows = left_feat.shape[0] // 2
    width = left_feat.shape[2]

    def keep_part(a, axis=0):
        count = a.shape[axis] // 2
        return lax.dynamic_slice_in_dim(a, core * count, count, axis)

    def give_part(a, axis=0):
        count = a.shape[axis] // 2
        return lax.dynamic_slice_in_dim(a, (1 - core) * count, count, axis)

    def swap(a):
        return lax.ppermute(a, "ch", [(0, 1), (1, 0)])

    def joined(own, other, axis):
        return jnp.where(core == 0, jnp.concatenate([own, other], axis),
                         jnp.concatenate([other, own], axis))

    def over_cols(a, step):
        pairs = [(i, i + step) for i in range(cols) if 0 <= i + step < cols]
        return lax.ppermute(a, "col", pairs)

    def crossed(a, step):
        pairs = [(2 * i + j, 2 * (i + step) + 1 - j)
                 for i in range(cols) if 0 <= i + step < cols for j in range(2)]
        return lax.ppermute(a, ("col", "ch"), pairs)

    def over_rows(a, step):
        pairs = [(i, i + step) for i in range(rows2) if 0 <= i + step < rows2]
        return lax.ppermute(a, ("row", "ch"), pairs)

    left_own, left_give = keep_part(left_feat), give_part(left_feat)
    right_own, right_give = keep_part(right_feat), give_part(right_feat)
    one_own = over_cols(right_own, 1)
    one_other = crossed(right_give, 1)
    left_other, right_other = swap(left_give), swap(right_give)
    left_all = jnp.concatenate([left_own, left_other], axis=1)
    left_one = over_cols(left_all, -1)
    two_own = over_cols(one_own, 1)
    two_other = over_cols(one_other, 1)
    left_two = over_cols(left_one, -1)

    maps = jnp.stack([grad_out, valid.astype(F32)])
    maps = joined(keep_part(maps, 1), swap(give_part(maps, 1)), 2)
    grad_map, keep = maps[0], maps[1]
    weights = refine_weights(w_first, w_middle, w_last, rows)

    rights = ((right_own, right_other), (one_own, one_other), (two_own, two_other))
    left = (left_own, left_other)
    field, top, bottom, stats = band_stats(offsets, left, rights, grad_map, keep)

    above, below = over_rows(bottom, 1), over_rows(top, -1)
    first = jnp.concatenate([above[:, :, :HALO], field[:, :, :HALO], below[:, :, :HALO]], axis=1)
    final = jnp.concatenate([a[:, :, width - HALO:] for a in (above, field, below)], axis=1)
    before, after = over_cols(final, 1), over_cols(first, -1)
    gap = jnp.zeros(after.shape[:2] + (SIDE - 2 * HALO,), F32)
    side = jnp.concatenate([after, gap, before], axis=2)
    flags = jnp.stack([band == 0, band == rows2 - 1, col == 0, col == cols - 1]).astype(jnp.int32)
    flags = jnp.concatenate([flags, offsets])
    refined, coef = refine(flags, field, above, below, side, stats, keep, weights, chans, hid)

    coef_one, coef_two = over_cols(coef, -1), over_cols(coef, -2)
    grad_left = left_grads(offsets, left, rights, coef)
    grad_left = joined(grad_left[0], swap(grad_left[1]), 0)
    offs = jnp.stack([offsets[0], coef_one[0, 5, 0].astype(jnp.int32),
                      coef_two[0, 5, 0].astype(jnp.int32)])
    grad_right = right_grads(offs, rights[0], left, left_one, left_two, (coef, coef_one, coef_two))
    grad_right = joined(grad_right[0], swap(grad_right[1]), 0)
    refined = joined(keep_part(refined, 1), swap(give_part(refined, 1)), 0)
    return (refined, grad_left, grad_right)


def solution(mesh):
    placed = (
        P(("slab", "row"), "ch", "col"),
        P(("slab", "row"), "ch", "col"),
        P(("slab", "col")),
        P(("slab", "row"), ("col", "ch")),
        P(),
        P(),
        P(),
        P(("slab", "row"), ("col", "ch")),
    )
    return jax.shard_map(
        shards,
        mesh=mesh,
        in_specs=placed,
        out_specs=(placed[3], placed[0], placed[0]),
        check_vma=False,
    )
```

```python
import functools
import math

import jax
import jax.numpy as jnp
import numpy as np
from jax import lax
from jax.experimental import pallas as pl
from jax.experimental.pallas import tpu as pltpu
from jax.sharding import PartitionSpec as P

DISP = 256
HALO = 4
LANES = 128
SIDE = 128
ALIGN = 16
NEG = -1e30
BAND = 400
GROUP = 4
F32 = jnp.float32
BF16 = jnp.bfloat16


def dot(a, b, dims=((1,), (0,))):
    return lax.dot_general(a, b, (dims, ((), ())), preferred_element_type=F32)


def band_tables(off):
    rem = (DISP + 1 - off) % ALIGN
    across = lax.broadcasted_iota(jnp.int32, (BAND, LANES), 1)
    down = lax.broadcasted_iota(jnp.int32, (BAND, LANES), 0)
    delta = across - down + (DISP - 1) + rem
    inside = (delta >= 0) & (delta < DISP)
    return delta.astype(F32) / DISP, jnp.where(inside, 0.0, NEG).astype(F32)


def band_start(off, block):
    rem = (DISP + 1 - off) % ALIGN
    return pl.multiple_of(LANES * block + DISP + 1 - off - rem, ALIGN)


def softmax_part(scores, lev, rate):
    top_score = jnp.max(scores, axis=0, keepdims=True)
    weight = jnp.exp2((scores - top_score) * rate)
    total = jnp.sum(weight, axis=0, keepdims=True)
    mean = jnp.sum(weight * lev, axis=0, keepdims=True) / total
    apart = lev - mean
    spread = jnp.sum(weight * apart * apart, axis=0, keepdims=True) / total
    return spread, top_score, mean, total


def early_body(chans, off_ref, lk, lo, r0k, r0o, r1k, r1o, lines, cost, level, mask):
    step = pl.program_id(0)
    rate = math.log2(math.e) / math.sqrt(chans)
    off = off_ref[0]
    width = lk.shape[2]

    @pl.when(step == 0)
    def _():
        lev, msk = band_tables(off)
        level[...] = lev
        mask[...] = msk
        cost[:width, :] = jnp.full((width, width), NEG, F32)
        cost[3 * width:, :] = jnp.full((cost.shape[0] - 3 * width, width), NEG, F32)

    @pl.loop(0, GROUP)
    def _(row):
        left = jnp.concatenate([lk[row], lo[row]], axis=0)
        for slot, (own, other) in enumerate(((r1k, r1o), (r0k, r0o))):
            right = jnp.concatenate([own[row], other[row]], axis=0)
            cost[(slot + 1) * width:(slot + 2) * width, :] = dot(right, left, ((0,), (0,)))
        line = step * GROUP + row
        for block in range(width // LANES):
            cols = slice(block * LANES, (block + 1) * LANES)
            scores = cost[pl.ds(band_start(off, block), BAND), cols] + mask[...]
            for at, value in enumerate(softmax_part(scores, level[...], rate)):
                lines[line, at:at + 1, cols] = value


def late_body(chans, off_ref, lk, lo, rk, ro, early, grad_ref, keep_ref,
              field, top, bottom, stats, level, mask, lines, planes):
    step = pl.program_id(0)
    rate = math.log2(math.e) / math.sqrt(chans)
    off = off_ref[0]
    width = lk.shape[2]

    @pl.when(step == 0)
    def _():
        across = lax.broadcasted_iota(jnp.int32, (width, width), 1)
        down = lax.broadcasted_iota(jnp.int32, (width, width), 0)
        delta = across - down + 2 * width - off
        level[...] = delta.astype(F32) / DISP
        mask[...] = jnp.where((delta >= 0) & (delta < DISP), 0.0, NEG).astype(F32)

    for row in range(GROUP):
        left = jnp.concatenate([lk[row], lo[row]], axis=0)
        right = jnp.concatenate([rk[row], ro[row]], axis=0)
        cost = dot(right, left, ((0,), (0,)))
        line = step * GROUP + row
        for block in range(width // LANES):
            cols = slice(block * LANES, (block + 1) * LANES)
            part = (slice(block * LANES, width), cols)
            for at, value in enumerate(softmax_part(cost[part] + mask[part], level[part], rate)):
                lines[line, at:at + 1, cols] = value

    rows = field.shape[1]

    @pl.when(step == pl.num_programs(0) - 1)
    def _():
        for line in range(rows):
            for at in range(4):
                planes[at, line:line + 1, :] = lines[line, at:at + 1, :]
                planes[at + 4, line:line + 1, :] = early[line, at:at + 1, :]
        top_score = jnp.maximum(planes[1], planes[5])
        mass_a = planes[3] * jnp.exp2((planes[1] - top_score) * rate)
        mass_b = planes[7] * jnp.exp2((planes[5] - top_score) * rate)
        share = 1.0 / (mass_a + mass_b)
        mass_a, mass_b = mass_a * share, mass_b * share
        gap = planes[6] - planes[2]
        mean = mass_a * planes[2] + mass_b * planes[6]
        spread = mass_a * planes[0] + mass_b * planes[4] + gap * gap * mass_a * mass_b
        keep = keep_ref[...]
        coarse = mean + off.astype(F32) / DISP
        for at, plane in enumerate((coarse, spread, top_score, mean, share)):
            stats[at] = plane
        field[0] = coarse * keep
        field[1] = spread * keep
        field[2] = grad_ref[...] * keep
        top[...] = field[:, :HALO, :]
        bottom[...] = field[:, rows - HALO:, :]


def group_spec(array):
    return pl.BlockSpec((GROUP,) + array.shape[1:], lambda i: (i, 0, 0))


def full_spec(shape):
    return pl.BlockSpec(shape, lambda i: (0,) * len(shape))


SMEM = pl.BlockSpec(memory_space=pltpu.SMEM)


def cost_of(flops, moved):
    return pl.CostEstimate(flops=flops, bytes_accessed=moved, transcendentals=0)


def early_stats(off, left, rights):
    rows, half, width = left[0].shape
    chans = 2 * half
    feats = list(left) + [part for pair in rights for part in pair]
    return pl.pallas_call(
        functools.partial(early_body, chans),
        name="early_stats",
        grid=(rows // GROUP,),
        in_specs=[SMEM] + [group_spec(a) for a in feats],
        out_specs=full_spec((rows, 8, width)),
        out_shape=jax.ShapeDtypeStruct((rows, 8, width), F32),
        scratch_shapes=[
            pltpu.VMEM((3 * width + ALIGN, width), F32),
            pltpu.VMEM((BAND, LANES), F32),
            pltpu.VMEM((BAND, LANES), F32),
        ],
        cost_estimate=cost_of(2 * rows * 3 * width * width * chans, rows * 3 * width * chans * 2),
    )(off, *feats)


def late_stats(off, left, right, early, grad_out, keep):
    rows, half, width = left[0].shape
    chans = 2 * half
    feats = list(left) + list(right)
    small = (rows, width)
    outs = ((3,) + small, (3, HALO, width), (3, HALO, width), (5,) + small)
    return pl.pallas_call(
        functools.partial(late_body, chans),
        name="late_stats",
        grid=(rows // GROUP,),
        in_specs=[SMEM] + [group_spec(a) for a in feats] + [full_spec(early.shape)]
        + [full_spec(small)] * 2,
        out_specs=[full_spec(s) for s in outs],
        out_shape=[jax.ShapeDtypeStruct(s, F32) for s in outs],
        scratch_shapes=[
            pltpu.VMEM((width, width), F32),
            pltpu.VMEM((width, width), F32),
            pltpu.VMEM((rows, 8, width), F32),
            pltpu.VMEM((8,) + small, F32),
        ],
        cost_estimate=cost_of(rows * 3 * width * width * chans, rows * 2 * width * chans * 2),
    )(off, *feats, early, grad_out, keep)


def left_body(chans, off_ref, lk, lo, r0k, r0o, r1k, r1o, r2k, r2o, coef, out_own, out_other,
              level, mask, tiles, cost, slopes):
    step = pl.program_id(0)
    rate = math.log2(math.e) / math.sqrt(chans)
    off = off_ref[0]
    width = lk.shape[2]
    parts = width // LANES
    depth = DISP + 2 * LANES
    span = depth + width - LANES
    skip = jnp.where(off < 3 * width - span, 3 * width - span, 0)

    @pl.when(step == 0)
    def _():
        across = lax.broadcasted_iota(jnp.int32, (depth, LANES), 1)
        down = lax.broadcasted_iota(jnp.int32, (depth, LANES), 0)
        delta = across - down + 2 * width - off - skip
        level[...] = delta.astype(F32) / DISP
        mask[...] = jnp.where((delta >= 0) & (delta < DISP), 0.0, NEG).astype(F32)
        slopes[...] = jnp.zeros(slopes.shape, BF16)

    for row in range(GROUP):
        for slot, (own, other) in enumerate(((r2k, r2o), (r1k, r1o), (r0k, r0o))):
            at = slice(slot * width, (slot + 1) * width)
            tiles[row, :chans // 2, at] = own[row]
            tiles[row, chans // 2:, at] = other[row]
    rights = [tiles[row, :, pl.ds(pl.multiple_of(skip, LANES), span)] for row in range(GROUP)]
    for row, right in enumerate(rights):
        left = jnp.concatenate([lk[row], lo[row]], axis=0)
        cost[row] = dot(right, left, ((0,), (0,)))
        at = step * GROUP + row
        for block in range(parts):
            cols = slice(block * LANES, (block + 1) * LANES)
            where = slice(block * LANES, block * LANES + depth)
            top_score, mean, one, two, three = (coef[at, f:f + 1, cols] for f in range(5))
            weight = jnp.exp2((cost[row, where, cols] + mask[...] - top_score) * rate)
            apart = level[...] - mean
            slopes[row, where, cols] = (weight * (apart * (one + two * apart) - three)).astype(BF16)
        total = dot(right, slopes[row])
        out_own[row] = total[:chans // 2].astype(BF16)
        out_other[row] = total[chans // 2:].astype(BF16)


def left_grads(off, left, rights, coef):
    rows, half, width = left[0].shape
    chans = 2 * half
    feats = list(left) + [part for pair in rights for part in pair]
    depth = DISP + 2 * LANES
    span = depth + width - LANES
    return pl.pallas_call(
        functools.partial(left_body, chans),
        name="left_grads",
        grid=(rows // GROUP,),
        in_specs=[SMEM] + [group_spec(a) for a in feats] + [full_spec(coef.shape)],
        out_specs=[group_spec(left[0])] * 2,
        out_shape=[jax.ShapeDtypeStruct(left[0].shape, BF16)] * 2,
        scratch_shapes=[
            pltpu.VMEM((depth, LANES), F32),
            pltpu.VMEM((depth, LANES), F32),
            pltpu.VMEM((GROUP, chans, 3 * width), BF16),
            pltpu.VMEM((GROUP, span, width), F32),
            pltpu.VMEM((GROUP, span, width), BF16),
        ],
        cost_estimate=cost_of(4 * rows * 3 * width * width * chans, rows * 5 * width * chans * 2),
    )(off, *feats, coef)


def right_body(chans, rk, ro, l0k, l0o, l1k, l1o, l2k, l2o, coef0, coef1, coef2,
               out_own, out_other, cost, slopes, mask):
    step = pl.program_id(0)
    rate = math.log2(math.e) / math.sqrt(chans)
    width = rk.shape[2]
    parts = width // LANES
    coefs = (coef0, coef1, coef2)
    across = lax.broadcasted_iota(jnp.int32, (LANES, LANES), 1)
    down = lax.broadcasted_iota(jnp.int32, (LANES, LANES), 0)
    blocks = [(tile, col, row) for tile in range(3) for col in range(parts) for row in range(parts)
              if -LANES < tile * width + (col - row) * LANES and
              tile * width + (col - row) * LANES - width < DISP + LANES]

    def spot(tile, col, row):
        return (slice(row * LANES, (row + 1) * LANES),
                slice(tile * width + col * LANES, tile * width + (col + 1) * LANES))

    def base_of(at, tile, col, row):
        cols = slice(col * LANES, (col + 1) * LANES)
        return (tile * width + (col - row) * LANES) - coefs[tile][at, 5:6, cols]

    @pl.when(step == 0)
    def _():
        slopes[...] = jnp.zeros(slopes.shape, BF16)
        for tile, col, row in blocks:
            delta = across - down + base_of(0, tile, col, row).astype(jnp.int32)
            inside = (delta >= 0) & (delta < DISP)
            mask[spot(tile, col, row)] = jnp.where(inside, 0.0, NEG).astype(F32)

    for line in range(GROUP):
        right = jnp.concatenate([rk[line], ro[line]], axis=0)
        lefts = [jnp.concatenate([own[line], other[line]], axis=0)
                 for own, other in ((l0k, l0o), (l1k, l1o), (l2k, l2o))]
        for tile, left in enumerate(lefts):
            cost[line, :, tile * width:(tile + 1) * width] = dot(right, left, ((0,), (0,)))
        at = step * GROUP + line
        table = (across - down).astype(F32) / DISP
        for tile, col, row in blocks:
            here = spot(tile, col, row)
            cols = slice(col * LANES, (col + 1) * LANES)
            top_score, mean, one, two, three = (coefs[tile][at, f:f + 1, cols] for f in range(5))
            weight = jnp.exp2((cost[(line,) + here] + mask[here] - top_score) * rate)
            apart = table - (mean - base_of(at, tile, col, row) / DISP)
            slopes[(line,) + here] = (weight * (apart * (one + two * apart) - three)).astype(BF16)
        total = sum(dot(left, slopes[line, :, tile * width:(tile + 1) * width], ((1,), (1,)))
                    for tile, left in enumerate(lefts))
        out_own[line] = total[:chans // 2].astype(BF16)
        out_other[line] = total[chans // 2:].astype(BF16)


def right_grads(right, lefts, coefs):
    rows, half, width = right[0].shape
    chans = 2 * half
    feats = list(right) + [part for pair in lefts for part in pair]
    return pl.pallas_call(
        functools.partial(right_body, chans),
        name="right_grads",
        grid=(rows // GROUP,),
        in_specs=[group_spec(a) for a in feats] + [full_spec(a.shape) for a in coefs],
        out_specs=[group_spec(right[0])] * 2,
        out_shape=[jax.ShapeDtypeStruct(right[0].shape, BF16)] * 2,
        scratch_shapes=[
            pltpu.VMEM((GROUP, width, 3 * width), F32),
            pltpu.VMEM((GROUP, width, 3 * width), BF16),
            pltpu.VMEM((width, 3 * width), F32),
        ],
        cost_estimate=cost_of(4 * rows * 3 * width * width * chans, rows * 5 * width * chans * 2),
    )(*feats, *coefs)


def split_halves(values):
    high = values.astype(BF16)
    return high, (values - high.astype(F32)).astype(BF16)


def fine_dot(weights, high, low):
    w_high, w_low = weights
    return dot(w_high, high) + dot(w_high, low) + dot(w_low, high)


def tap_rows(values):
    last = values.shape[1] - 1
    return jnp.concatenate([pltpu.roll(values, 1, 1), values, pltpu.roll(values, last, 1)], axis=0)


def merge_taps(stacked):
    count, lanes = stacked.shape[0] // 3, stacked.shape[1]
    return (pltpu.roll(stacked[:count], 1, 1) + stacked[count:2 * count]
            + pltpu.roll(stacked[2 * count:], lanes - 1, 1))


def refine_body(chans, hid, flags, field, above, below, side, stats, keep_ref,
                w_one, w_two, w_three, w_three_back, w_two_back, w_one_back,
                refined, coef, wide, one_high, one_low, slope_one,
                two_high, two_low, slope_two, g_two_high, g_two_low, g_one_high, g_one_low):
    rows, width = field.shape[1:]
    ext = rows + 2 * HALO
    lanes = width + SIDE
    for f in range(3):
        base = f * ext
        wide[base:base + HALO, :width] = above[f]
        wide[base + HALO:base + HALO + rows, :width] = field[f]
        wide[base + HALO + rows:base + ext, :width] = below[f]
        wide[base:base + ext, width:] = side[f]

    def present(first, count):
        line = first + lax.broadcasted_iota(jnp.int32, (count * hid, lanes), 0) // hid
        lane = lax.broadcasted_iota(jnp.int32, (count * hid, lanes), 1)
        low = HALO * flags[0]
        high = ext - HALO * flags[1]
        start = lanes - (SIDE // 2) * (1 - flags[2])
        end = width + (SIDE // 2) * (1 - flags[3])
        return (line >= low) & (line < high) & ((lane < end) | (lane >= start))

    def gate(values):
        return 1.0 / (1.0 + jnp.exp(-values))

    def activate(values, first, count, high_ref, low_ref, slope_ref, at):
        sig = gate(values)
        ok = present(first, count)
        hidden = jnp.where(ok, values * sig, 0.0)
        slope_ref[at] = jnp.where(ok, sig * (1.0 + values * (1.0 - sig)), 0.0)
        high_ref[at], low_ref[at] = split_halves(hidden)

    piece = 6
    taps = split_halves(tap_rows(wide[:2 * ext, :]))
    for part in range(ext // piece):
        at = slice(part * piece * hid, (part + 1) * piece * hid)
        values = fine_dot(split_halves(w_one[at, :]), *taps)
        activate(values, part * piece, piece, one_high, one_low, slope_one, at)

    count = ext - 4
    wt = split_halves(w_two[...])
    piece = w_two.shape[0] // (3 * hid)
    for part in range(count // piece):
        source = slice((part * piece + 1) * hid, (part * piece + 1) * hid + w_two.shape[1])
        values = merge_taps(fine_dot(wt, one_high[source], one_low[source]))
        at = slice(part * piece * hid, (part + 1) * piece * hid)
        activate(values, part * piece + 2, piece, two_high, two_low, slope_two, at)

    inner = slice(hid, (count - 1) * hid)
    out = merge_taps(fine_dot(split_halves(w_three[...]), two_high[inner], two_low[inner]))
    keep = keep_ref[...]
    refined[...] = keep * (stats[0] + out[:, :width])

    taps = split_halves(tap_rows(wide[2 * ext:, :]))
    for part in range(count // piece):
        at = slice(part * piece * hid, (part + 1) * piece * hid)
        grads = fine_dot(split_halves(w_three_back[at, :]), *taps) * slope_two[at]
        g_two_high[at], g_two_low[at] = split_halves(grads)

    wt = split_halves(w_two_back[...])
    piece = w_two_back.shape[0] // (3 * hid)
    for part in range((count - 2) // piece):
        source = slice(part * piece * hid, part * piece * hid + w_two_back.shape[1])
        at = slice(part * piece * hid, (part + 1) * piece * hid)
        over = slice((part * piece + 3) * hid, (part * piece + 3 + piece) * hid)
        grads = merge_taps(fine_dot(wt, g_two_high[source], g_two_low[source])) * slope_one[over]
        g_one_high[at], g_one_low[at] = split_halves(grads)

    back = merge_taps(fine_dot(split_halves(w_one_back[...]), g_one_high[...], g_one_low[...]))
    for_coarse = field[2] + back[:rows, :width] * keep
    for_spread = back[rows:, :width] * keep
    scale = stats[4] / math.sqrt(chans)
    planes = (stats[2], stats[3], for_coarse * scale, for_spread * scale,
              for_spread * stats[1] * scale, jnp.full((rows, width), flags[4], jnp.int32).astype(F32))
    coef[...] = jnp.zeros(coef.shape, F32)
    for at, plane in enumerate(planes):
        for line in range(rows):
            coef[line, at:at + 1, :] = plane[line:line + 1, :]


def near(out_rows, in_rows, shift):
    gap = np.arange(in_rows)[None, :] - np.arange(out_rows)[:, None] + shift
    return [(gap == tap).astype(np.float32) for tap in range(3)]


def expand(weights, out_rows, in_rows, shift, order):
    table = near(out_rows, in_rows, shift)
    full = sum(jnp.asarray(table[tap])[None, :, None, :, None] * weights[tap][:, None, :, None, :]
               for tap in range(3))
    return jnp.transpose(full, order)


def refine_weights(w_first, w_middle, w_last, rows):
    ext = rows + 2 * HALO
    hid, ins = w_first.shape[2:]

    def turned(w):
        return jnp.transpose(w[::-1, ::-1], (0, 1, 3, 2))

    one = expand(w_first, ext, ext, 1, (1, 2, 0, 4, 3)).reshape(ext * hid, 3 * ins * ext)
    two = expand(w_middle, 5, 7, 0, (0, 1, 2, 3, 4)).reshape(3 * 5 * hid, 7 * hid)
    three = expand(w_last, rows, rows + 2, 0, (0, 1, 2, 3, 4)).reshape(3 * rows, (rows + 2) * hid)
    three_back = expand(turned(w_last), ext - 4, ext, -1, (1, 2, 0, 4, 3)).reshape(
        (ext - 4) * hid, 3 * ext)
    two_back = expand(turned(w_middle), 6, 8, 0, (0, 1, 2, 3, 4)).reshape(3 * 6 * hid, 8 * hid)
    one_back = expand(turned(w_first), rows, rows + 2, 0, (0, 2, 1, 3, 4)).reshape(
        3 * ins * rows, (rows + 2) * hid)
    return one, two, three, three_back, two_back, one_back


def refine(flags, field, above, below, side, stats, keep, weights, chans, hid):
    rows, width = field.shape[1:]
    ext, lanes = rows + 2 * HALO, width + SIDE
    small = (rows, width)
    vmem = pl.BlockSpec(memory_space=pltpu.VMEM)
    outs = (small, (rows, 8, width))

    def both(count):
        return [pltpu.VMEM((count * hid, lanes), BF16)] * 2

    def single(count):
        return [pltpu.VMEM((count * hid, lanes), F32)]

    return pl.pallas_call(
        functools.partial(refine_body, chans, hid),
        name="refine",
        in_specs=[SMEM] + [vmem] * 12,
        out_specs=[vmem] * 2,
        out_shape=[jax.ShapeDtypeStruct(s, F32) for s in outs],
        scratch_shapes=[pltpu.VMEM((3 * ext, lanes), F32)] + both(ext) + single(ext)
        + both(ext - 4) + single(ext - 4) + both(ext - 4) + both(ext - 6),
        cost_estimate=cost_of(4 * 10 ** 9, 8 * 10 ** 6),
    )(flags, field, above, below, side, stats, keep, *weights)


def shards(left_feat, right_feat, offsets, valid, w_first, w_middle, w_last, grad_out):
    cols, rows2 = lax.axis_size("col"), lax.axis_size("row") * lax.axis_size("ch")
    col, core = lax.axis_index("col"), lax.axis_index("ch")
    band = lax.axis_index("row") * lax.axis_size("ch") + core
    chans = left_feat.shape[1] * lax.axis_size("ch")
    hid = w_first.shape[2]
    rows = left_feat.shape[0] // 2
    width = left_feat.shape[2]

    def keep_part(a, axis=0):
        count = a.shape[axis] // 2
        return lax.dynamic_slice_in_dim(a, core * count, count, axis)

    def give_part(a, axis=0):
        count = a.shape[axis] // 2
        return lax.dynamic_slice_in_dim(a, (1 - core) * count, count, axis)

    def swap(a):
        return lax.ppermute(a, "ch", [(0, 1), (1, 0)])

    def joined(own, other, axis):
        return jnp.where(core == 0, jnp.concatenate([own, other], axis),
                         jnp.concatenate([other, own], axis))

    def over_cols(a, step):
        pairs = [(i, i + step) for i in range(cols) if 0 <= i + step < cols]
        return lax.ppermute(a, "col", pairs)

    def crossed(a, step):
        pairs = [(2 * i + j, 2 * (i + step) + 1 - j)
                 for i in range(cols) if 0 <= i + step < cols for j in range(2)]
        return lax.ppermute(a, ("col", "ch"), pairs)

    def over_rows(a, step):
        pairs = [(i, i + step) for i in range(rows2) if 0 <= i + step < rows2]
        return lax.ppermute(a, ("row", "ch"), pairs)

    left_own, left_give = keep_part(left_feat), give_part(left_feat)
    right_own, right_give = keep_part(right_feat), give_part(right_feat)
    right_one = (over_cols(right_own, 1), crossed(right_give, 1))
    left_one = (over_cols(left_own, -1), crossed(left_give, -1))
    left = (left_own, swap(left_give))
    right = (right_own, swap(right_give))
    right_two = tuple(over_cols(a, 1) for a in right_one)
    left_two = tuple(over_cols(a, -1) for a in left_one)

    maps = jnp.stack([grad_out, valid.astype(F32)])
    maps = joined(keep_part(maps, 1), swap(give_part(maps, 1)), 2)
    grad_map, keep = maps[0], maps[1]
    weights = refine_weights(w_first, w_middle, w_last, rows)

    early = early_stats(offsets, left, (right, right_one))
    early, right_two, left_two, weights, grad_map, keep = lax.optimization_barrier(
        (early, right_two, left_two, weights, grad_map, keep))
    field, top, bottom, stats = late_stats(offsets, left, right_two, early, grad_map, keep)
    rights = (right, right_one, right_two)

    above, below = over_rows(bottom, 1), over_rows(top, -1)
    first = jnp.concatenate([above[:, :, :HALO], field[:, :, :HALO], below[:, :, :HALO]], axis=1)
    final = jnp.concatenate([a[:, :, width - HALO:] for a in (above, field, below)], axis=1)
    before, after = over_cols(final, 1), over_cols(first, -1)
    gap = jnp.zeros(after.shape[:2] + (SIDE - 2 * HALO,), F32)
    side = jnp.concatenate([after, gap, before], axis=2)
    flags = jnp.stack([band == 0, band == rows2 - 1, col == 0, col == cols - 1]).astype(jnp.int32)
    flags = jnp.concatenate([flags, offsets])
    refined, coef = refine(flags, field, above, below, side, stats, keep, weights, chans, hid)

    coef_one, coef_two = over_cols(coef, -1), over_cols(coef, -2)
    grad_left = left_grads(offsets, left, rights, coef)
    grad_left = joined(grad_left[0], swap(grad_left[1]), 0)
    grad_right = right_grads(right, (left, left_one, left_two), (coef, coef_one, coef_two))
    grad_right = joined(grad_right[0], swap(grad_right[1]), 0)
    refined = joined(keep_part(refined, 1), swap(give_part(refined, 1)), 0)
    return (refined, grad_left, grad_right)


def solution(mesh):
    placed = (
        P(("slab", "row"), "ch", "col"),
        P(("slab", "row"), "ch", "col"),
        P(("slab", "col")),
        P(("slab", "row"), ("col", "ch")),
        P(),
        P(),
        P(),
        P(("slab", "row"), ("col", "ch")),
    )
    return jax.shard_map(
        shards,
        mesh=mesh,
        in_specs=placed,
        out_specs=(placed[3], placed[0], placed[0]),
        check_vma=False,
    )
```
